32 devices in a mesh: parts: 2 (over x), tm: 8 (over z, y), stn: 2 (over core).
Axes of the slice: x: 2, y: 2, z: 4, core: 2. Of those that a mesh axis runs over, the one named last changes fastest.
Arguments:
- voltages: bfloat16 [256, 2, 32, 2, 2048], P(('parts', 'stn'), None, 'tm'), parts along dimension 0, may hold values from -6 to 6
- filter_taps: float32 [16, 2048], replicated, may hold values from -1.5 to 1.5
- use_mask: int32 [512, 8], P('parts'), parts along dimension 0, may hold values 0 or 1
- block_index: int32 [512, 8], P('parts'), parts along dimension 0, may hold values from 0 to 127
- weight_blocks: bfloat16 [128, 512], P('tm'), may hold values from -0.5 to 0.5
Outputs:
- power: float32 [2048, 32, 512], P('stn', 'tm', 'parts'), parts along dimension 2
The draws below stay inside these ranges and needn't reach their ends.
There are 2 independent parts, one for each index of `parts`. The reference program is written for one: setup_inputs(seed, part) draws one part's arguments, and reference() takes and returns one part's arrays. A program takes and returns all parts, laid end to end along the dimension named above; an argument that names none is the same for every part. Nothing has to cross between parts.
All inputs are finite; a program needn't handle non-finite values.
Results may differ from the reference program's by a relative error of at most 0.008.
Values may be sent and summed in bfloat16 or wider, within the bound.
A program may use at most 192 MiB of HBM per device.

```python
import math
import jax
import jax.numpy as jnp
from jax import lax

C = 2048
P_SIZE = 64
Q = 32
BEAMS = 256
TAPS = 16
SB = 16
G = 16
S_DEV = 64
STATIONS = 128
FRAMES = 32
NB = 8
NWB = 128


def touch_ends(entries, own_key, low, largest):
    longest = entries.shape.index(max(entries.shape))
    spots = []
    for shift in (0, 1):
        where = [jax.random.randint(jax.random.fold_in(own_key, axis), (), 0, length) for axis, length in enumerate(entries.shape)]
        where[longest] = (where[longest] + shift) % entries.shape[longest]
        spots.append(tuple(where))
    return entries.at[spots[0]].set(low).at[spots[1]].set(largest)


def levels(own_key, dims, shards, smallest, top_value):
    level = 1.0
    for dim, shards_of in shards:
        heights = jax.random.uniform(jax.random.fold_in(jax.random.fold_in(own_key, 6), dim), (shards_of,), jnp.float32, smallest / len(shards), top_value / len(shards))
        level = level * jnp.repeat(jnp.exp(heights), dims[dim] // shards_of).reshape((-1,) + (1,) * (len(dims) - 1 - dim))
    return level


def bell_draw(rng, dims, deviation, most, pieces=(), kind=jnp.bfloat16):
    loudness = levels(rng, dims, pieces, -0.22, 0.18) if pieces else 1.0
    result = jax.random.normal(rng, dims, jnp.float32) * deviation * loudness
    return jnp.minimum(jnp.maximum(result, -most), most).astype(kind)


def setup_inputs(seed: int = 0, part: int = 0) -> dict:
    splits = jax.random.split(jax.random.key(seed), 6)
    part_keys = jax.random.split(jax.random.fold_in(splits[5], part), 6)
    voltages = bell_draw(part_keys[0], (STATIONS, 2, FRAMES, 2, C), 1.0, 6.0, ((0, 2), (2, 8)))
    filter_taps = bell_draw(splits[1], (TAPS, C), 0.25, 1.5, (), jnp.float32)
    use_mask = touch_ends((jax.random.randint(part_keys[2], (BEAMS, NB), 0, 2) < 1).astype(jnp.int32), jax.random.fold_in(part_keys[2], 1), 0, 1)
    block_index = touch_ends(jax.random.randint(part_keys[3], (BEAMS, NB), 0, NWB), jax.random.fold_in(part_keys[3], 1), 0, NWB - 1).astype(jnp.int32)
    weight_blocks = bell_draw(splits[4], (NWB, G * 2 * SB), (2 * S_DEV) ** -0.5, 0.5, ((0, 8),))
    return dict(voltages=voltages, filter_taps=filter_taps, use_mask=use_mask, block_index=block_index, weight_blocks=weight_blocks)


def transform_tables(first_size, second_size):
    full_size = first_size * second_size
    first_range = jnp.arange(first_size, dtype=jnp.int32)
    second_range = jnp.arange(second_size, dtype=jnp.int32)
    first_angle = (first_range[:, None] * first_range[None, :] % first_size).astype(jnp.float32) * (2.0 * math.pi / first_size)
    cosine_first = jnp.cos(first_angle)
    sine_first = jnp.sin(first_angle)
    section_one = jnp.stack([jnp.stack([cosine_first, -sine_first], axis=1), jnp.stack([sine_first, cosine_first], axis=1)], axis=0)
    second_angle = (second_range[:, None] * second_range[None, :] % second_size).astype(jnp.float32) * (2.0 * math.pi / second_size)
    cosine_second = jnp.cos(second_angle)
    sine_second = jnp.sin(second_angle)
    section_two = jnp.stack([jnp.stack([cosine_second, sine_second], axis=-1), jnp.stack([-sine_second, cosine_second], axis=-1)], axis=1)
    section_two = section_two.reshape(2 * second_size, 2 * second_size)
    twist_angle = (second_range[:, None] * first_range[None, :] % full_size).astype(jnp.float32) * (2.0 * math.pi / full_size)
    return (section_one.astype(jnp.bfloat16), jnp.cos(twist_angle), jnp.sin(twist_angle), section_two.astype(jnp.bfloat16))

def filter_frames(window, filter_taps, frame_count):
    history = filter_taps.shape[0] - 1
    shape_out = window.shape[:2] + (frame_count,) + window.shape[3:]
    summed = jnp.zeros(shape_out, jnp.float32)
    for tap_index in range(filter_taps.shape[0]):
        sliced = lax.slice_in_dim(window, history - tap_index, history - tap_index + frame_count, axis=2)
        summed = summed + filter_taps[tap_index] * sliced.astype(jnp.float32)
    return summed.astype(jnp.bfloat16)

def channelize(filtered, tables):
    section_one, twist_cos, twist_sin, section_two = tables
    first_size = section_one.shape[1]
    second_size = twist_cos.shape[0]
    station_count, frame_count = (filtered.shape[0], filtered.shape[2])
    reshaped = filtered.reshape(station_count, 2, frame_count, 2, first_size, second_size)
    first_section = jnp.einsum('spfrae,raob->spfeob', reshaped.astype(jnp.float32), section_one.astype(jnp.float32))
    real_part = first_section[:, :, :, :, 0, :]
    imag_part = first_section[:, :, :, :, 1, :]
    norm_factor = 1.0 / math.sqrt(first_size * second_size)
    twist_real = (real_part * twist_cos + imag_part * twist_sin) * norm_factor
    twist_imag = (imag_part * twist_cos - real_part * twist_sin) * norm_factor
    twiddled = jnp.stack([twist_real, twist_imag], axis=-2).astype(jnp.bfloat16)
    twiddled = twiddled.reshape(station_count, 2, frame_count, 2 * second_size, first_size)
    spectra = jnp.einsum('dk,spfkb->spfdb', section_two.astype(jnp.float32), twiddled.astype(jnp.float32))
    return spectra.astype(jnp.bfloat16).reshape(station_count, 2, frame_count, second_size, 2, first_size)

def beam_matrix(use_rows, picked):
    beam_count, block_count = use_rows.shape
    shaped = picked.reshape(beam_count, block_count, G, 2, SB) * use_rows.astype(jnp.bfloat16)[:, :, None, None, None]
    real_part = shaped[:, :, :, 0, :].transpose(2, 1, 3, 0).reshape(G, block_count * SB, beam_count)
    imag_part = shaped[:, :, :, 1, :].transpose(2, 1, 3, 0).reshape(G, block_count * SB, beam_count)
    upper_rows = jnp.stack([real_part, imag_part], axis=2)
    lower_rows = jnp.stack([-imag_part, real_part], axis=2)
    return jnp.stack([upper_rows, lower_rows], axis=1)

def form_beams(row_block, weights):
    row_count = row_block.shape[0]
    group_count = weights.shape[0]
    reshaped = row_block.reshape(group_count, -1, row_block.shape[2]).astype(jnp.float32)
    matrices = weights.reshape(group_count, row_block.shape[2], -1).astype(jnp.float32)
    product = jnp.einsum('gmk,gkn->gmn', reshaped, matrices)
    return product.reshape(row_count, -1)

def detect(summed):
    shaped = summed.reshape(summed.shape[0], 4, -1)
    return lax.optimization_barrier(jnp.sum(shaped * shaped, axis=1))

def reference(voltages, filter_taps, use_mask, block_index, weight_blocks):
    tables = transform_tables(P_SIZE, Q)
    history = TAPS - 1

    def per_station(station):
        window = jnp.pad(station[None], ((0, 0), (0, 0), (history, 0), (0, 0), (0, 0)))
        filtered = filter_frames(window, filter_taps, FRAMES)
        return channelize(filtered, tables)[0]
    spectra = lax.map(per_station, voltages)
    turned = spectra.transpose(2, 3, 5, 1, 4, 0).reshape(FRAMES, C, 2, 2, STATIONS)
    picked = weight_blocks[block_index]
    matrix = beam_matrix(use_mask, picked)
    member_count = STATIONS // S_DEV

    def per_frame(frame_rows):
        summed = jnp.zeros((C, 4 * BEAMS), jnp.float32)
        for member in range(member_count):
            low = member * S_DEV
            row_block = frame_rows[:, :, :, low:low + S_DEV].reshape(C, 2, 2 * S_DEV)
            weights = matrix[:, :, low:low + S_DEV]
            partial_value = form_beams(row_block, weights).astype(jnp.bfloat16)
            partial_value = lax.optimization_barrier(partial_value)
            summed = summed + partial_value.astype(jnp.float32)
        return detect(summed)
    detected = lax.map(per_frame, turned)
    return detected.transpose(1, 0, 2)
```

```python
import functools
import math

import jax
import jax.numpy as jnp
from jax import lax
from jax.experimental import pallas as pl
from jax.experimental.pallas import tpu as pltpu
from jax.sharding import PartitionSpec as P

SB = 16
G = 16
LANES = 128
MESH = pl.DeviceIdType.MESH


def share_stations_kernel(size, v_ref, w_ref, out_ref, rows_ref, hold, hold_w, local, send, recv, send_w, recv_w):
    me = lax.axis_index("tm")
    barrier = pltpu.get_barrier_semaphore()
    for step in range(1, size):
        pl.semaphore_signal(barrier, inc=1, device_id={"tm": lax.rem(me + step, size)}, device_id_type=MESH)
    pl.semaphore_wait(barrier, size - 1)
    copies = []
    for step in range(1, size):
        to = lax.rem(me + step, size)
        copies.append(pltpu.make_async_remote_copy(
            src_ref=w_ref, dst_ref=rows_ref.at[me], send_sem=send_w.at[step], recv_sem=recv_w.at[step],
            device_id={"tm": to}, device_id_type=MESH))
        copies.append(pltpu.make_async_remote_copy(
            src_ref=v_ref.at[to], dst_ref=out_ref.at[me], send_sem=send.at[step], recv_sem=recv.at[step],
            device_id={"tm": to}, device_id_type=MESH))
    for copy in copies:
        copy.start()
    for source, middle, target, index in ((v_ref.at[me], hold, out_ref.at[me], 0), (w_ref, hold_w, rows_ref.at[me], 1)):
        copy = pltpu.make_async_copy(source, middle, local.at[index])
        copy.start()
        copy.wait()
        copy = pltpu.make_async_copy(middle, target, local.at[index])
        copy.start()
        copy.wait()
    for copy in copies:
        copy.wait()


def share_stations(blocks, weight_rows):
    size = blocks.shape[0]
    return pl.pallas_call(
        functools.partial(share_stations_kernel, size),
        out_shape=(jax.ShapeDtypeStruct(blocks.shape, blocks.dtype),
                   jax.ShapeDtypeStruct((size,) + weight_rows.shape, weight_rows.dtype)),
        in_specs=[pl.BlockSpec(memory_space=pl.ANY)] * 2,
        out_specs=[pl.BlockSpec(memory_space=pl.ANY)] * 2,
        scratch_shapes=[
            pltpu.VMEM(blocks.shape[1:], blocks.dtype), pltpu.VMEM(weight_rows.shape, weight_rows.dtype),
            pltpu.SemaphoreType.DMA((2,)),
            pltpu.SemaphoreType.DMA((size,)), pltpu.SemaphoreType.DMA((size,)),
            pltpu.SemaphoreType.DMA((size,)), pltpu.SemaphoreType.DMA((size,)),
        ],
        compiler_params=pltpu.CompilerParams(collective_id=0, has_side_effects=True),
        name="share_stations",
    )(blocks, weight_rows)


def return_frames_kernel(size, z_ref, out_ref, hold, local, send, recv):
    me = lax.axis_index("tm")
    core = lax.axis_index("stn")
    others = [(step, side) for step in range(size) for side in range(2) if step or side]
    targets = [(lax.rem(me + step, size), lax.rem(core + side, 2)) for step, side in others]
    barrier = pltpu.get_barrier_semaphore()
    for to, to_core in targets:
        pl.semaphore_signal(barrier, inc=1, device_id={"tm": to, "stn": to_core}, device_id_type=MESH)
    pl.semaphore_wait(barrier, len(others))
    slot = core * size + me
    copies = []
    for index, (to, to_core) in enumerate(targets):
        copies.append(pltpu.make_async_remote_copy(
            src_ref=z_ref.at[to, to_core], dst_ref=out_ref.at[slot], send_sem=send.at[index], recv_sem=recv.at[index],
            device_id={"tm": to, "stn": to_core}, device_id_type=MESH))
    for copy in copies:
        copy.start()
    copy = pltpu.make_async_copy(z_ref.at[me, core], hold, local)
    copy.start()
    copy.wait()
    copy = pltpu.make_async_copy(hold, out_ref.at[slot], local)
    copy.start()
    copy.wait()
    for copy in copies:
        copy.wait()


def return_frames(blocks):
    size = blocks.shape[0]
    return pl.pallas_call(
        functools.partial(return_frames_kernel, size),
        out_shape=jax.ShapeDtypeStruct((2 * size,) + blocks.shape[2:], blocks.dtype),
        in_specs=[pl.BlockSpec(memory_space=pl.ANY)],
        out_specs=pl.BlockSpec(memory_space=pl.ANY),
        scratch_shapes=[
            pltpu.VMEM(blocks.shape[2:], blocks.dtype), pltpu.SemaphoreType.DMA,
            pltpu.SemaphoreType.DMA((2 * size - 1,)), pltpu.SemaphoreType.DMA((2 * size - 1,)),
        ],
        compiler_params=pltpu.CompilerParams(collective_id=1, has_side_effects=True),
        name="return_frames",
    )(blocks)


def transform_tables(first, stations):
    full = first * LANES
    a = jnp.arange(first, dtype=jnp.int32)
    l = jnp.arange(LANES, dtype=jnp.int32)
    angle = (a[:, None] * a[None, :] % first).astype(jnp.float32) * (2.0 * math.pi / first)
    cos, sin = jnp.cos(angle), jnp.sin(angle)
    one = jnp.stack([jnp.stack([cos, sin], axis=1), jnp.stack([-sin, cos], axis=1)], axis=0)
    eye = jnp.eye(stations, dtype=jnp.float32)
    one = one[:, :, None, None] * eye[None, None, :, :, None, None]
    one = one.reshape(2 * first * stations, stations * 2 * first)
    angle = (l[:, None] * l[None, :] % LANES).astype(jnp.float32) * (2.0 * math.pi / LANES)
    cos, sin = jnp.cos(angle), jnp.sin(angle)
    two = jnp.stack([jnp.stack([cos, -sin], axis=0), jnp.stack([sin, cos], axis=0)], axis=0)
    two = two.reshape(2, 2, LANES, 2, 8, 8).transpose(0, 2, 3, 4, 1, 5)
    two = two.reshape(2 * LANES, 2 * LANES)
    angle = (a[:, None] * l[None, :] % full).astype(jnp.float32) * (2.0 * math.pi / full)
    norm = 1.0 / math.sqrt(full)
    twist_cos = jnp.repeat(jnp.cos(angle) * norm, stations, axis=0)
    twist_sin = jnp.repeat(jnp.sin(angle) * norm, stations, axis=0)
    return one.astype(jnp.bfloat16), two.astype(jnp.bfloat16), twist_cos, twist_sin


def channelize_kernel(x_ref, taps_ref, one_ref, two_ref, cos_ref, sin_ref, z_ref, window, held):
    size, stations, _, frames, _, first, _ = x_ref.shape
    taps = taps_ref.shape[0]
    block = pl.program_id(1)

    @pl.when(block == 0)
    def _():
        window[0:taps] = jnp.zeros((taps,) + window.shape[1:], window.dtype)

        def fill(t, carry):
            for f in range(frames):
                window[taps + t * frames + f] = x_ref[t, :, 0, f]
            return carry
        lax.fori_loop(0, size, fill, 0)

    base = block * frames + 1

    def filter_rows(index, carry):
        s = index // 2
        r = lax.rem(index, 2)
        sums = [None] * frames
        for m in range(frames + taps - 1):
            x = window[base + m, s, r].astype(jnp.float32)
            for f in range(frames):
                k = f + taps - 1 - m
                if 0 <= k < taps:
                    term = taps_ref[k] * x
                    sums[f] = term if sums[f] is None else sums[f] + term
        for f in range(frames):
            held[f, pl.ds(pl.multiple_of(index * first, first), first)] = sums[f].astype(held.dtype)
        return carry
    lax.fori_loop(0, 2 * stations, filter_rows, 0)

    rows = first * stations
    for f in range(frames):
        y = jnp.dot(one_ref[...], held[f], preferred_element_type=jnp.float32)
        re, im = y[:rows], y[rows:]
        cos, sin = cos_ref[...], sin_ref[...]
        turned = jnp.concatenate([re * cos + im * sin, im * cos - re * sin], axis=1).astype(jnp.bfloat16)
        z = jnp.dot(turned, two_ref[...], preferred_element_type=jnp.float32).astype(z_ref.dtype)
        for h in range(2):
            z_ref[0, h, 0, f] = z[:, h * LANES:(h + 1) * LANES]


def channelize(x, taps, tables):
    size, stations, pols, frames, _, first, _ = x.shape
    one, two, cos, sin = tables
    rows = first * stations
    fixed = lambda a: pl.BlockSpec(a.shape, lambda p, j: (0,) * a.ndim)
    taps = taps.reshape(taps.shape[0], first, LANES)
    return pl.pallas_call(
        channelize_kernel,
        grid=(pols, size),
        out_shape=jax.ShapeDtypeStruct((size, 2, pols, frames, rows, LANES), jnp.bfloat16),
        in_specs=[
            pl.BlockSpec((size, stations, 1, frames, 2, first, LANES), lambda p, j: (0, 0, p, 0, 0, 0, 0)),
            fixed(taps), fixed(one), fixed(two), fixed(cos), fixed(sin),
        ],
        out_specs=pl.BlockSpec((1, 2, 1, frames, rows, LANES), lambda p, j: (j, 0, p, 0, 0, 0)),
        scratch_shapes=[
            pltpu.VMEM((size * frames + taps.shape[0], stations, 2, first, LANES), jnp.bfloat16),
            pltpu.VMEM((frames, 2 * rows, LANES), jnp.bfloat16),
        ],
        name="channelize",
    )(x, taps, one, two, cos, sin)


def beams_kernel(s_ref, w_ref, out_ref, turned):
    sources, pols, _, first, stations, _ = s_ref.shape
    groups, depth, wide = w_ref.shape
    beams = wide // 2
    for p in range(pols):
        def turn(c1, carry):
            tile = s_ref[:, p, 0, c1].reshape(depth, LANES)
            tile = tile.astype(jnp.float32).T.astype(jnp.bfloat16)
            for g in range(groups):
                turned[p, g, c1] = tile[g * 16:(g + 1) * 16]
            return carry
        lax.fori_loop(0, first, turn, 0)

    def group(g, carry):
        power = None
        for p in range(pols):
            rows = turned[p, g].reshape(first * 16, depth)
            y = jnp.dot(rows, w_ref[g], preferred_element_type=jnp.float32).reshape(first, 2, 8, wide)
            re = y[:, 0, :, :beams] - y[:, 1, :, beams:]
            im = y[:, 0, :, beams:] + y[:, 1, :, :beams]
            term = re * re + im * im
            power = term if power is None else power + term
        out_ref[0, g] = power
        return carry
    lax.fori_loop(0, groups, group, 0)


def form_beams(spectra, weights):
    sources, pols, frames, first, stations, _ = spectra.shape
    groups, depth, wide = weights.shape
    return pl.pallas_call(
        beams_kernel,
        grid=(frames,),
        out_shape=jax.ShapeDtypeStruct((frames, groups, first, 8, wide // 2), jnp.float32),
        in_specs=[
            pl.BlockSpec((sources, pols, 1, first, stations, LANES), lambda f: (0, 0, f, 0, 0, 0)),
            pl.BlockSpec(weights.shape, lambda f: (0, 0, 0)),
        ],
        out_specs=pl.BlockSpec((1, groups, first, 8, wide // 2), lambda f: (f, 0, 0, 0, 0)),
        scratch_shapes=[pltpu.VMEM((pols, groups, first, 16, depth), jnp.bfloat16)],
        name="form_beams",
    )(spectra, weights)


def beam_weights(use_mask, block_index, rows, half, groups):
    beams, blocks = block_index.shape
    ids = jnp.arange(rows.shape[0], dtype=jnp.int32)
    index = block_index.T.reshape(-1)
    mask = use_mask.T.reshape(-1)
    onehot = jnp.where(index[:, None] == ids[None, :], mask[:, None], 0).astype(jnp.bfloat16)
    width = groups * 2 * SB
    mine = lax.dynamic_slice_in_dim(rows, half * width, width, 1)
    picked = lax.dot_general(mine, onehot, (((0,), (1,)), ((), ())), preferred_element_type=jnp.float32)
    picked = picked.astype(jnp.bfloat16).reshape(groups, 2, SB, blocks, beams)
    return picked.transpose(0, 3, 2, 1, 4).reshape(groups, blocks * SB, 2 * beams)


def body(voltages, filter_taps, use_mask, block_index, weight_blocks):
    stations, pols, frames, _, channels = voltages.shape
    size = lax.axis_size("tm")
    first = channels // LANES
    share = stations // size
    blocks = voltages.reshape(size, share, pols, frames, 2, first, LANES)
    x, rows = share_stations(blocks, weight_blocks)
    tables = transform_tables(first, share)
    z = channelize(x, filter_taps, tables)
    spectra = return_frames(z)
    spectra = spectra.reshape(2 * size, pols, frames, first, share, LANES)
    groups = G // 2
    weights = beam_weights(use_mask, block_index, rows.reshape(-1, rows.shape[-1]), lax.axis_index("stn"), groups)
    power = form_beams(spectra, weights)
    return power.transpose(1, 3, 2, 0, 4).reshape(channels // 2, frames, -1)


def solution(mesh):
    in_specs = (
        P(("parts", "stn"), None, "tm", None, None),
        P(),
        P("parts", None),
        P("parts", None),
        P("tm", None),
    )
    out_specs = P("stn", "tm", "parts")
    return jax.shard_map(body, mesh=mesh, in_specs=in_specs, out_specs=out_specs, check_vma=False)
```

```python
import functools
import math

import jax
import jax.numpy as jnp
from jax import lax
from jax.experimental import pallas as pl
from jax.experimental.pallas import tpu as pltpu
from jax.sharding import PartitionSpec as P

SB = 16
G = 16
LANES = 128
MESH = pl.DeviceIdType.MESH


def transform_tables(first, stations):
    full = first * LANES
    a = jnp.arange(first, dtype=jnp.int32)
    l = jnp.arange(LANES, dtype=jnp.int32)
    angle = (a[:, None] * a[None, :] % first).astype(jnp.float32) * (2.0 * math.pi / first)
    cos, sin = jnp.cos(angle), jnp.sin(angle)
    one = jnp.stack([jnp.stack([cos, sin], axis=1), jnp.stack([-sin, cos], axis=1)], axis=0)
    eye = jnp.eye(stations, dtype=jnp.float32)
    one = one[:, :, None, None] * eye[None, None, :, :, None, None]
    one = one.reshape(2 * first * stations, stations * 2 * first)
    angle = (l[:, None] * l[None, :] % LANES).astype(jnp.float32) * (2.0 * math.pi / LANES)
    cos, sin = jnp.cos(angle), jnp.sin(angle)
    two = jnp.stack([jnp.stack([cos, -sin], axis=0), jnp.stack([sin, cos], axis=0)], axis=0)
    two = two.reshape(2, 2, LANES, 2, 8, 8).transpose(0, 2, 3, 4, 1, 5)
    two = two.reshape(2 * LANES, 2 * LANES)
    angle = (a[:, None] * l[None, :] % full).astype(jnp.float32) * (2.0 * math.pi / full)
    norm = 1.0 / math.sqrt(full)
    twist_cos = jnp.repeat(jnp.cos(angle) * norm, stations, axis=0)
    twist_sin = jnp.repeat(jnp.sin(angle) * norm, stations, axis=0)
    return one.astype(jnp.bfloat16), two.astype(jnp.bfloat16), twist_cos, twist_sin


def kernel(size, v_ref, rows_ref, onehot_ref, taps_ref, one_ref, two_ref, cos_ref, sin_ref, out_ref,
           x, window, held, z, r, table, weights, turned,
           local, send_w, recv_w, send_x, recv_x, send_z, recv_z):
    me = lax.axis_index("tm")
    core = lax.axis_index("stn")
    pols, _, stations, frames, _, first, _ = x.shape
    taps = taps_ref.shape[0]
    rows = first * stations
    groups, depth, wide = weights.shape
    beams = wide // 2
    slot = core * size + me

    barrier = pltpu.get_barrier_semaphore()
    for step in range(size):
        for side in range(2):
            if step or side:
                pl.semaphore_signal(
                    barrier, inc=1, device_id={"tm": lax.rem(me + step, size), "stn": lax.rem(core + side, 2)},
                    device_id_type=MESH)
    pl.semaphore_wait(barrier, 2 * size - 1)

    def weight_copy(step):
        return pltpu.make_async_remote_copy(
            src_ref=rows_ref, dst_ref=table.at[me], send_sem=send_w.at[step], recv_sem=recv_w.at[step],
            device_id={"tm": lax.rem(me + step, size)}, device_id_type=MESH)

    def voltage_copy(p, step):
        to = lax.rem(me + step, size)
        return pltpu.make_async_remote_copy(
            src_ref=v_ref.at[to, :, p], dst_ref=x.at[p, me], send_sem=send_x.at[p, step], recv_sem=recv_x.at[p, step],
            device_id={"tm": to}, device_id_type=MESH)

    def spectra_copy(p, step, side):
        to = lax.rem(me + step, size)
        to_core = lax.rem(core + side, 2)
        return pltpu.make_async_remote_copy(
            src_ref=z.at[p, to, to_core], dst_ref=r.at[p, slot],
            send_sem=send_z.at[p, step, side], recv_sem=recv_z.at[p, step, side],
            device_id={"tm": to, "stn": to_core}, device_id_type=MESH)

    for step in range(1, size):
        weight_copy(step).start()
    for p in range(pols):
        for step in range(1, size):
            voltage_copy(p, step).start()
    own = [pltpu.make_async_copy(v_ref.at[me, :, p], x.at[p, me], local.at[p]) for p in range(pols)]
    own.append(pltpu.make_async_copy(rows_ref, table.at[me], local.at[pols]))
    for copy in own:
        copy.start()

    window[0:taps] = jnp.zeros((taps,) + window.shape[1:], window.dtype)
    for step in range(1, size):
        weight_copy(step).wait()
    own[pols].wait()
    width = groups * 2 * SB
    mine = table[:, :, pl.ds(pl.multiple_of(core * width, width), width)].reshape(-1, width)
    mine = mine.astype(jnp.float32).T.astype(jnp.bfloat16)

    def pick(q, carry):
        picked = jnp.dot(mine, onehot_ref[q], preferred_element_type=jnp.float32).astype(jnp.bfloat16)
        for g in range(groups):
            for part in range(2):
                low = (2 * g + part) * SB
                weights[g, pl.ds(pl.multiple_of(q * SB, SB), SB), part * beams:(part + 1) * beams] = picked[low:low + SB]
        return carry
    lax.fori_loop(0, depth // SB, pick, 0)

    for p in range(pols):
        for step in range(1, size):
            voltage_copy(p, step).wait_recv()
        own[p].wait()

        def fill(t, carry):
            for f in range(frames):
                window[taps + t * frames + f] = x[p, t, :, f]
            return carry
        lax.fori_loop(0, size, fill, 0)

        def block(step, carry):
            to = lax.rem(me + step, size)
            base = to * frames + 1

            def filter_rows(index, carry):
                s = index // 2
                part = lax.rem(index, 2)
                sums = [None] * frames
                for m in range(frames + taps - 1):
                    sample = window[base + m, s, part].astype(jnp.float32)
                    for f in range(frames):
                        k = f + taps - 1 - m
                        if 0 <= k < taps:
                            term = taps_ref[k] * sample
                            sums[f] = term if sums[f] is None else sums[f] + term
                for f in range(frames):
                    held[f, pl.ds(pl.multiple_of(index * first, first), first)] = sums[f].astype(held.dtype)
                return carry
            lax.fori_loop(0, 2 * stations, filter_rows, 0)

            def transform(f, carry):
                y = jnp.dot(one_ref[...], held[f], preferred_element_type=jnp.float32)
                re, im = y[:rows], y[rows:]
                cos, sin = cos_ref[...], sin_ref[...]
                twisted = jnp.concatenate([re * cos + im * sin, im * cos - re * sin], axis=1).astype(jnp.bfloat16)
                spectra = jnp.dot(twisted, two_ref[...], preferred_element_type=jnp.float32)
                for h in range(2):
                    z[p, to, h, f] = spectra[:, h * LANES:(h + 1) * LANES].reshape(first, stations, LANES).astype(z.dtype)
                return carry
            lax.fori_loop(0, frames, transform, 0)

            @pl.when(step < size)
            def _():
                spectra_copy(p, lax.rem(step, size), 0).start()
            spectra_copy(p, lax.rem(step, size), 1).start()
            return carry
        lax.fori_loop(1, size + 1, block, 0)
        copy = pltpu.make_async_copy(z.at[p, me, core], r.at[p, slot], local.at[p])
        copy.start()
        copy.wait()

    for p in range(pols):
        for step in range(size):
            for side in range(2):
                if step or side:
                    spectra_copy(p, step, side).wait_recv()

        def frame(f, carry):
            def turn(c1, carry):
                tile = r[p, :, f, c1].reshape(depth, LANES)
                tile = tile.astype(jnp.float32).T.astype(jnp.bfloat16)
                for g in range(groups):
                    turned[g, c1] = tile[g * 16:(g + 1) * 16]
                return carry
            lax.fori_loop(0, first, turn, 0)

            def group(g, carry):
                y = jnp.dot(turned[g].reshape(first * 16, depth), weights[g], preferred_element_type=jnp.float32)
                y = y.reshape(first, 2, 8, wide)
                re = y[:, 0, :, :beams] - y[:, 1, :, beams:]
                im = y[:, 0, :, beams:] + y[:, 1, :, :beams]
                term = re * re + im * im
                out_ref[f, g] = term if p == 0 else out_ref[f, g] + term
                return carry
            lax.fori_loop(0, groups, group, 0)
            return carry
        lax.fori_loop(0, frames, frame, 0)

    for p in range(pols):
        for step in range(size):
            if step:
                voltage_copy(p, step).wait_send()
            for side in range(2):
                if step or side:
                    spectra_copy(p, step, side).wait_send()


def fused(v, weight_rows, onehot, taps, tables):
    size, stations, pols, frames, _, first, _ = v.shape
    groups = G // 2
    blocks, _, beams = onehot.shape
    depth = blocks * SB
    rows = first * stations
    taps = taps.reshape(taps.shape[0], first, LANES)
    bf16 = jnp.bfloat16
    dma = pltpu.SemaphoreType.DMA
    vmem = pl.BlockSpec(memory_space=pltpu.VMEM)
    hbm = pl.BlockSpec(memory_space=pl.ANY)
    return pl.pallas_call(
        functools.partial(kernel, size),
        out_shape=jax.ShapeDtypeStruct((frames, groups, first, 8, beams), jnp.float32),
        in_specs=[hbm, vmem] + [vmem] * 6,
        out_specs=vmem,
        scratch_shapes=[
            pltpu.VMEM((pols, size, stations, frames, 2, first, LANES), bf16),
            pltpu.VMEM((size * frames + taps.shape[0], stations, 2, first, LANES), bf16),
            pltpu.VMEM((frames, 2 * rows, LANES), bf16),
            pltpu.VMEM((pols, size, 2, frames, first, stations, LANES), bf16),
            pltpu.VMEM((pols, 2 * size, frames, first, stations, LANES), bf16),
            pltpu.VMEM((size,) + weight_rows.shape, bf16),
            pltpu.VMEM((groups, depth, 2 * beams), bf16),
            pltpu.VMEM((groups, first, 16, depth), bf16),
            dma((pols + 1,)), dma((size,)), dma((size,)),
            dma((pols, size)), dma((pols, size)), dma((pols, size, 2)), dma((pols, size, 2)),
        ],
        compiler_params=pltpu.CompilerParams(collective_id=0, has_side_effects=True, vmem_limit_bytes=60 << 20),
        name="fused_beams",
    )(v, weight_rows, onehot, taps, *tables)


def body(voltages, filter_taps, use_mask, block_index, weight_blocks):
    stations, pols, frames, _, channels = voltages.shape
    size = lax.axis_size("tm")
    first = channels // LANES
    share = stations // size
    blocks = voltages.reshape(size, share, pols, frames, 2, first, LANES)
    ids = jnp.arange(size * weight_blocks.shape[0], dtype=jnp.int32)
    onehot = jnp.where(
        block_index.T[:, None, :] == ids[None, :, None], use_mask.T[:, None, :], 0).astype(jnp.bfloat16)
    power = fused(blocks, weight_blocks, onehot, filter_taps, transform_tables(first, share))
    return power.transpose(1, 3, 2, 0, 4).reshape(channels // 2, frames, -1)


def solution(mesh):
    in_specs = (
        P(("parts", "stn"), None, "tm", None, None),
        P(),
        P("parts", None),
        P("parts", None),
        P("tm", None),
    )
    out_specs = P("stn", "tm", "parts")
    return jax.shard_map(body, mesh=mesh, in_specs=in_specs, out_specs=out_specs, check_vma=False)
```

```python
import functools
import math

import jax
import jax.numpy as jnp
import numpy as np
from jax import lax
from jax.experimental import pallas as pl
from jax.experimental.pallas import tpu as pltpu
from jax.sharding import PartitionSpec as P

SB = 16
G = 16
LANES = 128
MESH = pl.DeviceIdType.MESH


def transform_tables(first, stations):
    full = first * LANES
    a = np.arange(first)
    l = np.arange(LANES)

    def waves(product, period):
        angle = (product % period).astype(np.float32) * np.float32(2.0 * math.pi / period)
        return np.cos(angle), np.sin(angle)

    cos, sin = waves(a[:, None] * a[None, :], first)
    one = np.stack([np.stack([cos, sin], axis=-1), np.stack([-sin, cos], axis=-1)], axis=0)
    eye = np.eye(stations, dtype=np.float32)
    one = one[:, :, None, None] * eye[None, None, :, :, None, None]
    one = one.reshape(2 * first * stations, stations * 2 * first)
    cos, sin = waves(l[:, None] * l[None, :], LANES)
    two = np.stack([np.stack([cos, -sin], axis=0), np.stack([sin, cos], axis=0)], axis=0)
    two = two.reshape(2, 2, LANES, 2, 8, 8).transpose(0, 2, 3, 4, 1, 5)
    two = two.reshape(2 * LANES, 2 * LANES)
    cos, sin = waves(a[:, None] * l[None, :], full)
    norm = np.float32(1.0 / math.sqrt(full))
    cos = np.repeat(cos * norm, stations, axis=0)
    sin = np.repeat(sin * norm, stations, axis=0)
    return jnp.asarray(one, jnp.bfloat16), jnp.asarray(two, jnp.bfloat16), jnp.asarray(cos), jnp.asarray(sin)


def kernel(size, v_ref, rows_ref, onehot_ref, taps_ref, one_ref, two_ref, cos_ref, sin_ref, out_ref,
           x, window, held, z, r, table, weights, turned, total,
           local, send_w, recv_w, send_x, recv_x, send_z, recv_z):
    me = lax.axis_index("tm")
    core = lax.axis_index("stn")
    pols, _, stations, frames, first, _ = x.shape
    first //= 2
    half = frames // 2
    taps = taps_ref.shape[0]
    rows = first * stations
    groups, depth, wide = weights.shape
    beams = wide // 2
    slot = core * size + me

    barrier = pltpu.get_barrier_semaphore()
    for step in range(size):
        for side in range(2):
            if step or side:
                pl.semaphore_signal(
                    barrier, inc=1, device_id={"tm": lax.rem(me + step, size), "stn": lax.rem(core + side, 2)},
                    device_id_type=MESH)
    pl.semaphore_wait(barrier, 2 * size - 1)

    def weight_copy(step):
        return pltpu.make_async_remote_copy(
            src_ref=rows_ref, dst_ref=table.at[me], send_sem=send_w.at[step], recv_sem=recv_w.at[step],
            device_id={"tm": lax.rem(me + step, size)}, device_id_type=MESH)

    def voltage_copy(p, step):
        to = lax.rem(me + step, size)
        return pltpu.make_async_remote_copy(
            src_ref=v_ref.at[to, :, p], dst_ref=x.at[p, me], send_sem=send_x.at[p, step], recv_sem=recv_x.at[p, step],
            device_id={"tm": to}, device_id_type=MESH)

    def spectra_copy(p, step, side, late):
        to = lax.rem(me + step, size)
        to_core = lax.rem(core + side, 2)
        return pltpu.make_async_remote_copy(
            src_ref=z.at[p, to, to_core, pl.ds(late * half, half)], dst_ref=r.at[p, slot, pl.ds(late * half, half)],
            send_sem=send_z.at[p, step, side, late], recv_sem=recv_z.at[p, step, side, late],
            device_id={"tm": to, "stn": to_core}, device_id_type=MESH)

    def send_spectra(p, step, late):
        @pl.when(step < size)
        def _():
            spectra_copy(p, lax.rem(step, size), 0, late).start()
        spectra_copy(p, lax.rem(step, size), 1, late).start()

    for step in range(1, size):
        weight_copy(step).start()
    for p in range(pols):
        for step in range(1, size):
            voltage_copy(p, step).start()
    own = [pltpu.make_async_copy(v_ref.at[me, :, p], x.at[p, me], local.at[p]) for p in range(pols)]
    own.append(pltpu.make_async_copy(rows_ref, table.at[me], local.at[pols]))
    for copy in own:
        copy.start()

    window[0:taps] = jnp.zeros((taps,) + window.shape[1:], window.dtype)
    for step in range(1, size):
        weight_copy(step).wait()
    own[pols].wait()
    width = groups * 2 * SB
    mine = table[:, :, pl.ds(pl.multiple_of(core * width, width), width)].reshape(-1, width)
    mine = mine.astype(jnp.float32).T.astype(jnp.bfloat16)

    def pick(q, carry):
        picked = jnp.dot(mine, onehot_ref[q], preferred_element_type=jnp.float32).astype(jnp.bfloat16)
        for g in range(groups):
            for part in range(2):
                low = (2 * g + part) * SB
                weights[g, pl.ds(pl.multiple_of(q * SB, SB), SB), part * beams:(part + 1) * beams] = picked[low:low + SB]
        return carry
    lax.fori_loop(0, depth // SB, pick, 0)

    for p in range(pols):
        for step in range(1, size):
            voltage_copy(p, step).wait_recv()
        own[p].wait()

        def fill(t, carry):
            for f in range(frames):
                window[taps + t * frames + f] = x[p, t, :, f]
            return carry
        lax.fori_loop(0, size, fill, 0)

        def block(step, carry):
            to = lax.rem(me + step, size)
            base = to * frames + 1

            def filter_rows(index, carry):
                s = index // 2
                part = lax.rem(index, 2)
                sums = [None] * frames
                for m in range(frames + taps - 1):
                    sample = window[base + m, s, pl.ds(pl.multiple_of(part * first, first), first)].astype(jnp.float32)
                    for f in range(frames):
                        k = f + taps - 1 - m
                        if 0 <= k < taps:
                            term = taps_ref[k, part] * sample
                            sums[f] = term if sums[f] is None else sums[f] + term
                for f in range(frames):
                    held[f, pl.ds(pl.multiple_of(index * first, first), first)] = sums[f].astype(held.dtype)
                return carry
            lax.fori_loop(0, 2 * stations, filter_rows, 0)

            def transform(f, carry):
                y = jnp.dot(one_ref[...], held[f], preferred_element_type=jnp.float32)
                re, im = y[:rows], y[rows:]
                cos, sin = cos_ref[...], sin_ref[...]
                twisted = jnp.concatenate([re * cos + im * sin, im * cos - re * sin], axis=1).astype(jnp.bfloat16)
                spectra = jnp.dot(twisted, two_ref[...], preferred_element_type=jnp.float32)
                for h in range(2):
                    z[p, to, h, f] = spectra[:, h * LANES:(h + 1) * LANES].reshape(first, stations, LANES).astype(z.dtype)
                return carry
            lax.fori_loop(0, frames, transform, 0)

            send_spectra(p, step, 0)
            if p < pols - 1:
                send_spectra(p, step, 1)
            return carry
        lax.fori_loop(1, size + 1, block, 0)
        if p == pols - 1:
            def rest(step, carry):
                send_spectra(p, step, 1)
                return carry
            lax.fori_loop(1, size + 1, rest, 0)
        copy = pltpu.make_async_copy(z.at[p, me, core], r.at[p, slot], local.at[p])
        copy.start()
        copy.wait()

    pieces = beams // LANES
    pitch = pieces * frames

    def frame_of(p, f):
        def turn(c1, carry):
            tile = r[p, :, f, c1].reshape(depth, LANES).T
            for g in range(groups):
                turned[g, c1] = tile[g * 16:(g + 1) * 16]
            return carry
        lax.fori_loop(0, first, turn, 0)

        def group(g, carry):
            y = jnp.dot(turned[g].reshape(first * 16, depth), weights[g], preferred_element_type=jnp.float32)
            y = y.reshape(first, 2, 8, wide)
            re = y[:, 0, :, :beams] - y[:, 1, :, beams:]
            im = y[:, 0, :, beams:] + y[:, 1, :, :beams]
            power = re * re + im * im
            if p > 0:
                power = total[f, g] + power
            if p < pols - 1:
                total[f, g] = power
            else:
                for c1 in range(first):
                    for piece in range(pieces):
                        row = g * (8 * first * pitch) + (c1 * pitch + piece * frames + f)
                        out_ref[pl.ds(row, 8, stride=first * pitch), :] = power[c1, :, piece * LANES:(piece + 1) * LANES]
            return carry
        lax.fori_loop(0, groups, group, 0)

    for p in range(pols):
        for late in range(2):
            for step in range(size):
                for side in range(2):
                    if step or side:
                        spectra_copy(p, step, side, late).wait_recv()

            def frame(f, carry):
                frame_of(p, f)
                return carry
            lax.fori_loop(late * half, (late + 1) * half, frame, 0)

    for p in range(pols):
        for step in range(size):
            if step:
                voltage_copy(p, step).wait_send()
            for side in range(2):
                if step or side:
                    for late in range(2):
                        spectra_copy(p, step, side, late).wait_send()


def fused(v, weight_rows, onehot, taps, tables):
    size, stations, pols, frames, first, _ = v.shape
    first //= 2
    groups = G // 2
    blocks, _, beams = onehot.shape
    depth = blocks * SB
    rows = first * stations
    taps = jnp.repeat(taps.reshape(taps.shape[0], first, LANES), 2, axis=1).reshape(-1, 2, first, LANES)
    bf16 = jnp.bfloat16
    dma = pltpu.SemaphoreType.DMA
    vmem = pl.BlockSpec(memory_space=pltpu.VMEM)
    hbm = pl.BlockSpec(memory_space=pl.ANY)
    return pl.pallas_call(
        functools.partial(kernel, size),
        out_shape=jax.ShapeDtypeStruct((groups * 8 * first * frames * beams // LANES, LANES), jnp.float32),
        in_specs=[hbm, vmem] + [vmem] * 6,
        out_specs=vmem,
        scratch_shapes=[
            pltpu.VMEM((pols, size, stations, frames, 2 * first, LANES), bf16),
            pltpu.VMEM((size * frames + taps.shape[0], stations, 2 * first, LANES), bf16),
            pltpu.VMEM((frames, 2 * rows, LANES), bf16),
            pltpu.VMEM((pols, size, 2, frames, first, stations, LANES), bf16),
            pltpu.VMEM((pols, 2 * size, frames, first, stations, LANES), bf16),
            pltpu.VMEM((size,) + weight_rows.shape, bf16),
            pltpu.VMEM((groups, depth, 2 * beams), bf16),
            pltpu.VMEM((groups, first, 16, depth), bf16),
            pltpu.VMEM((frames, groups, first, 8, beams), jnp.float32),
            dma((pols + 1,)), dma((size,)), dma((size,)),
            dma((pols, size)), dma((pols, size)), dma((pols, size, 2, 2)), dma((pols, size, 2, 2)),
        ],
        compiler_params=pltpu.CompilerParams(collective_id=0, has_side_effects=True, vmem_limit_bytes=60 << 20),
        name="fused_beams",
    )(v, weight_rows, onehot, taps, *tables)


def body(voltages, filter_taps, use_mask, block_index, weight_blocks):
    stations, pols, frames, _, channels = voltages.shape
    size = lax.axis_size("tm")
    first = channels // LANES
    share = stations // size
    blocks = voltages.reshape(size, share, pols, frames, 2, first, LANES).swapaxes(-3, -2)
    blocks = blocks.reshape(size, share, pols, frames, 2 * first, LANES)
    ids = jnp.arange(size * weight_blocks.shape[0], dtype=jnp.int32)
    onehot = jnp.where(
        block_index.T[:, None, :] == ids[None, :, None], use_mask.T[:, None, :], 0).astype(jnp.bfloat16)
    beams = block_index.shape[0]
    power = fused(blocks, weight_blocks, onehot, filter_taps, transform_tables(first, share))
    power = power.reshape(channels // 2, beams // LANES, frames, LANES)
    return power.swapaxes(1, 2).reshape(channels // 2, frames, beams)


def solution(mesh):
    in_specs = (
        P(("parts", "stn"), None, "tm", None, None),
        P(),
        P("parts", None),
        P("parts", None),
        P("tm", None),
    )
    out_specs = P("stn", "tm", "parts")
    return jax.shard_map(body, mesh=mesh, in_specs=in_specs, out_specs=out_specs, check_vma=False)
```
